32 devices in a mesh: tok: 4 (over y, x), hid: 8 (over z, core).
Axes of the slice: x: 2, y: 2, z: 4, core: 2. Of those that a mesh axis runs over, the one named last changes fastest.
Arguments:
- tokens: bfloat16 [6144, 6144], P('tok', 'hid'), may hold values from -6 to 6
- cotangent: bfloat16 [6144, 6144], P('tok', 'hid'), may hold values from -6 to 6
- expert_choice: int32 [6144, 2], P('tok'), may hold values from 0 to 7, as said below
- router: bfloat16 [8, 6144], replicated, may hold values from -0.078125 to 0.078125
- gate_up: bfloat16 [6144, 2, 8192], P('tok', None, 'hid'), may hold values from -0.109375 to 0.109375
- w_down: bfloat16 [6144, 8192], P('tok', 'hid'), may hold values from -0.0625 to 0.0625
Outputs:
- grad_tokens: bfloat16 [6144, 6144], P('tok', 'hid')
- d_combine: float32 [6144, 2], P('tok')
- d_gate_up: float32 [6144, 2, 8192], P('tok', None, 'hid')
- d_down: float32 [6144, 8192], P('tok', 'hid')
The draws below stay inside these ranges and needn't reach their ends.
Inputs may be any that keep to these rules, and one draw needn't show every extreme that they name: `expert_choice`: each row names 2 different experts. In every aligned block of 1536 rows at most 432 rows name expert 0 and at least half of 432 do; some block has exactly 432.
All inputs are finite; a program needn't handle non-finite values.
Results may differ from the reference program's by a relative error of at most 0.017.
Values may be sent and summed in bfloat16 or wider, within the bound.
A program may use at most 128 MiB of HBM per device.

```python
import jax
import jax.numpy as jnp
from jax import lax

D = 6144
FF = 8192
EXPERTS = 8
TOK_GROUP = 1536
CAP = 432
TOKENS = 6144
N_TOK = 4


def draw_expert_choice(key, part):
    streams = jax.random.split(jax.random.fold_in(key, 17), 6)
    blocks = TOKENS // TOK_GROUP
    counts = jax.random.randint(streams[0], (blocks,), CAP // 2, CAP + 1)
    fullest = jax.random.randint(streams[1], (), 0, blocks)
    counts = jnp.where(jnp.arange(blocks) == fullest, CAP, counts)
    orders = jax.vmap(lambda block_key: jax.random.permutation(block_key, TOK_GROUP))(jax.random.split(streams[2], blocks))
    chosen = (orders < counts[:, None]).reshape(TOKENS)
    leading = jax.random.randint(streams[3], (TOKENS,), 1, EXPERTS)
    offset = jax.random.randint(streams[4], (TOKENS,), 1, EXPERTS - 1)
    trailing = 1 + (leading - 1 + offset) % (EXPERTS - 1)
    column = jax.random.randint(streams[5], (TOKENS,), 0, 2)
    left_entry = jnp.where(chosen, jnp.where(column == 0, 0, leading), leading)
    right_entry = jnp.where(chosen, jnp.where(column == 0, leading, 0), trailing)
    return jnp.stack([left_entry, right_entry], axis=1).astype(jnp.int32)


def raised(result, key, source, target, shards_of, factor):
    owner, partner = [(jnp.arange(result.shape[position]) // (result.shape[position] // shards_of)).reshape([-1 if axis == position else 1 for axis in range(result.ndim)]) for position in (source, target)]
    chosen = jax.random.permutation(key, shards_of)[partner]
    strong = (owner == chosen) | (owner == (partner + shards_of // 2) % shards_of)
    return jnp.where(strong, factor * result, result)


def levels(rng, dims, pieces, low, high):
    def one(axis_at, blocks):
        steps = jax.random.uniform(jax.random.fold_in(jax.random.fold_in(rng, 6), axis_at), (blocks,), jnp.float32, low / len(pieces), high / len(pieces))
        return jnp.repeat(jnp.exp(steps), dims[axis_at] // blocks).reshape((-1,) + (1,) * (len(dims) - axis_at - 1))

    gain = one(*pieces[0])
    for cut in pieces[1:]:
        gain = gain * one(*cut)
    return gain


def normal_values(key, shape, width, bound, cuts=(), kind=jnp.bfloat16):
    entries = width * jax.random.normal(key, shape, jnp.float32)
    if cuts:
        entries = entries * levels(key, shape, cuts, -0.22, 0.18)
    return jnp.clip(entries, -bound, bound).astype(kind)


def noise_with(rng, shape, deviation, bound, cuts, heavy, kind=jnp.bfloat16):
    drawn = deviation * jax.random.normal(rng, shape, jnp.float32)
    if cuts:
        drawn = drawn * levels(rng, shape, cuts, -0.22, 0.18)
    return jnp.clip(raised(drawn, jax.random.fold_in(rng, 3), *heavy), -bound, bound).astype(kind)


def setup_inputs(seed: int = 0) -> dict:
    seeds = jax.random.split(jax.random.key(seed), 7)
    tokens = noise_with(seeds[0], (TOKENS, D), 1.0, 6.0, ((0, 4), (1, 8)), (0, 1, 8, 2.0))
    cotangent = noise_with(seeds[1], (TOKENS, D), 1.0, 6.0, ((0, 4), (1, 8)), (0, 1, 8, 2.0))
    expert_choice = draw_expert_choice(jax.random.fold_in(seeds[6], 71), 0)
    router = normal_values(seeds[3], (EXPERTS, D), D ** -0.5, 0.078125)
    gate_up = noise_with(seeds[4], (D, 2, FF), D ** -0.5, 0.109375, ((0, 4), (2, 8)), (2, 0, 8, 2.0))
    w_down = normal_values(seeds[5], (D, FF), FF ** -0.5, 0.0625, ((0, 4), (1, 8)))
    return dict(tokens=tokens, cotangent=cotangent, expert_choice=expert_choice, router=router, gate_up=gate_up, w_down=w_down)


def silu_pair(pre):
    sigma = jax.nn.sigmoid(pre)
    return pre * sigma, sigma * (1.0 + pre * (1.0 - sigma))


def rounded_add(total, term):
    return total + lax.optimization_barrier(term.astype(jnp.bfloat16)).astype(jnp.float32)


def reference(tokens, cotangent, expert_choice, router, gate_up, w_down):
    logits = jnp.dot(tokens, router.T, preferred_element_type=jnp.float32)
    first = expert_choice[:, 0]
    second = expert_choice[:, 1]
    in_first = first == 0
    in_second = second == 0
    routed = jnp.logical_or(in_first, in_second)
    other = first + second
    labels = jnp.arange(EXPERTS, dtype=jnp.int32)
    other_logit = jnp.sum(jnp.where(other[:, None] == labels[None, :], logits, 0.0), axis=1)
    gating = jnp.where(routed, jax.nn.sigmoid(logits[:, 0] - other_logit), 0.0)
    flags = routed.astype(jnp.int32).reshape(N_TOK, TOK_GROUP)
    slot_rank = jnp.cumsum(flags, axis=1) - flags
    slot_ids = jnp.arange(CAP, dtype=jnp.int32)
    placed = jnp.logical_and(flags[:, None, :] > 0, slot_rank[:, None, :] == slot_ids[None, :, None])
    dispatch = placed.astype(jnp.float32)
    grouped_in = tokens.astype(jnp.float32).reshape(N_TOK, TOK_GROUP, D)
    grouped_cot = cotangent.astype(jnp.float32).reshape(N_TOK, TOK_GROUP, D)
    expert_in = jnp.einsum("kcr,krd->kcd", dispatch, grouped_in, precision=lax.Precision.HIGHEST).astype(jnp.bfloat16)
    expert_cot = jnp.einsum("kcr,krd->kcd", dispatch, grouped_cot, precision=lax.Precision.HIGHEST).astype(jnp.bfloat16)
    slot_gate = jnp.sum(dispatch * gating.reshape(N_TOK, 1, TOK_GROUP), axis=2)
    weights_in = gate_up.reshape(D, 2 * FF)
    grad_in = jnp.zeros((D, 2 * FF), jnp.float32)
    grad_out = jnp.zeros((D, FF), jnp.float32)
    back_rows = []
    score_rows = []
    for group in range(N_TOK):
        rows_in = expert_in[group]
        rows_cot = expert_cot[group]
        scale = slot_gate[group][:, None]
        joined = jnp.dot(rows_in, weights_in, preferred_element_type=jnp.float32)
        gate_pre = joined[:, :FF]
        up_pre = joined[:, FF:]
        raw = jnp.dot(rows_cot, w_down, preferred_element_type=jnp.float32)
        active, slope = silu_pair(gate_pre)
        product = active * up_pre
        scaled = (scale * product).astype(jnp.bfloat16)
        score_rows.append(jnp.sum(product * raw, axis=1))
        upstream = scale * raw
        grads_mid = jnp.concatenate([(upstream * up_pre * slope).astype(jnp.bfloat16), (upstream * active).astype(jnp.bfloat16)], axis=1)
        grad_in = rounded_add(grad_in, jnp.dot(rows_in.T, grads_mid, preferred_element_type=jnp.float32))
        grad_out = rounded_add(grad_out, jnp.dot(rows_cot.T, scaled, preferred_element_type=jnp.float32))
        back_rows.append(jnp.dot(grads_mid, weights_in.T, preferred_element_type=jnp.float32))
    back = jnp.stack(back_rows)
    scores = jnp.stack(score_rows)
    safe = jnp.minimum(slot_rank, CAP - 1).astype(jnp.int32)
    picked = jax.vmap(lambda rows, index: jnp.take(rows, index, axis=0))(back, safe).reshape(TOKENS, D)
    routed_flat = flags.reshape(TOKENS) > 0
    grad_tokens = jnp.where(routed_flat[:, None], picked, 0.0).astype(jnp.bfloat16)
    picked_score = jax.vmap(lambda rows, index: jnp.take(rows, index, axis=0))(scores, safe).reshape(TOKENS)
    token_score = jnp.where(routed, picked_score, 0.0)
    d_combine = jnp.stack([jnp.where(in_first, token_score, 0.0), jnp.where(in_second, token_score, 0.0)], axis=1)
    return grad_tokens, d_combine, grad_in.reshape(D, 2, FF), grad_out
```

```python
import jax
import jax.numpy as jnp
from jax import lax
from jax.sharding import PartitionSpec as P

CAP = 432


def silu_pair(pre):
    sigma = jax.nn.sigmoid(pre)
    return (pre * sigma, sigma * (1.0 + pre * (1.0 - sigma)))


def contract_rows(left, right):
    return lax.dot_general(
        left, right, (((0,), (0,)), ((), ())), preferred_element_type=jnp.float32
    )


def contract_cols(left, right):
    return lax.dot_general(
        left, right, (((1,), (1,)), ((), ())), preferred_element_type=jnp.float32
    )


def swap(value, bit):
    count = lax.axis_size("tok")
    return lax.ppermute(value, "tok", [(k, k ^ bit) for k in range(count)])


def tok_sum(parts, bits, wire):
    held = dict(parts)
    for bit in bits:
        sent = [j for j in held if j & bit]
        arrived = {j ^ bit: swap(held[j].astype(wire), bit) for j in sent}
        held = {j: held[j] + arrived[j].astype(jnp.float32) for j in held if not j & bit}
    return held[0]


def tok_gather(own, bits):
    held = {0: own}
    for bit in bits:
        held.update({j | bit: swap(held[j], bit) for j in list(held)})
    return [held[j] for j in range(lax.axis_size("tok"))]


def local(tokens, cotangent, expert_choice, router, gate_up, w_down):
    n_tok = lax.axis_size("tok")
    n_hid = lax.axis_size("hid")
    share = n_hid // n_tok
    local_cols = tokens.shape[1]
    weight_rows, hidden_local = w_down.shape
    half = hidden_local // 2
    ups = [1 << b for b in range((n_tok - 1).bit_length())]
    downs = ups[::-1]
    first = expert_choice[:, 0]
    second = expert_choice[:, 1]
    in_first = first == 0
    in_second = second == 0
    routed = jnp.logical_or(in_first, in_second)
    flags = routed.astype(jnp.int32)
    slot_rank = jnp.cumsum(flags) - flags
    slot_ids = jnp.arange(CAP, dtype=jnp.int32)
    placed = jnp.logical_and(routed[None, :], slot_rank[None, :] == slot_ids[:, None])
    one_hot = placed.astype(jnp.bfloat16)
    forth = [
        (k * n_hid + t * share + c, t * n_hid + (k ^ t) * share + c)
        for k in range(n_tok)
        for t in range(n_tok)
        for c in range(share)
    ]
    back_pairs = [(b, a) for a, b in forth]

    def dispatch(values):
        picked = jnp.dot(one_hot, values, preferred_element_type=jnp.float32).astype(jnp.bfloat16)
        return lax.ppermute(picked, ("tok", "hid"), forth)

    def spread(moved):
        pieces = lax.all_gather(moved, "hid", axis=0)
        pieces = pieces.reshape(n_tok, share, CAP, local_cols).transpose(0, 2, 1, 3)
        return pieces.reshape(n_tok * CAP, weight_rows)

    moved_in = dispatch(tokens)
    moved_cot = dispatch(cotangent)
    rows_in = spread(moved_in)
    rows_cot = spread(moved_cot)
    w_gate = gate_up[:, 0, :]
    w_up = gate_up[:, 1, :]
    order = sorted(range(n_tok), key=lambda j: -j)

    def products(rows, weights):
        return {
            j: jnp.dot(rows[j * CAP : (j + 1) * CAP], weights, preferred_element_type=jnp.float32)
            for j in order
        }

    router_cols = lax.dynamic_slice_in_dim(
        router, lax.axis_index("tok") * weight_rows, weight_rows, 1
    )
    logit_parts = contract_cols(router_cols, rows_in)
    logits = tok_sum(
        {j: logit_parts[:, j * CAP : (j + 1) * CAP] for j in order}, ups, jnp.float32
    )
    gate_pre = tok_sum(products(rows_in, w_gate), ups, jnp.bfloat16)
    up_pre = tok_sum(products(rows_in, w_up), downs, jnp.bfloat16)
    raw = jnp.concatenate(
        [
            tok_sum(products(rows_cot, w_down[:, :half]), ups, jnp.bfloat16),
            tok_sum(products(rows_cot, w_down[:, half:]), downs, jnp.bfloat16),
        ],
        axis=1,
    )
    slot_other = jnp.sum(jnp.where(placed, (first + second)[None, :], 0), axis=1)
    filled = jnp.any(placed, axis=1)
    labels = jnp.arange(logits.shape[0], dtype=jnp.int32)
    other_logit = jnp.sum(jnp.where(slot_other[None, :] == labels[:, None], logits, 0.0), axis=0)
    slot_gate = jnp.where(filled, jax.nn.sigmoid(logits[0] - other_logit), 0.0)

    active, slope = silu_pair(gate_pre)
    product = active * up_pre
    scale = slot_gate[:, None]
    scaled = (scale * product).astype(jnp.bfloat16)
    score_part = jnp.sum(product * raw, axis=1)
    upstream = scale * raw
    grad_gate = tok_gather((upstream * up_pre * slope).astype(jnp.bfloat16), ups)
    grad_up = tok_gather((upstream * active).astype(jnp.bfloat16), downs)
    scores = lax.psum(score_part, "hid")
    scaled_left = tok_gather(scaled[:, :half], ups)
    scaled_right = tok_gather(scaled[:, half:], downs)

    backs = [
        (contract_cols(grad_gate[j], w_gate) + contract_cols(grad_up[j], w_up)).astype(jnp.bfloat16)
        for j in range(n_tok)
    ]
    shares = jnp.stack(
        [
            backs[j][:, c * local_cols : (c + 1) * local_cols]
            for j in range(n_tok)
            for c in range(share)
        ]
    )
    reduced = lax.psum_scatter(shares, "hid", scatter_dimension=0, tiled=False)
    back_cols = lax.ppermute(reduced, ("tok", "hid"), back_pairs)
    grad_tokens = contract_rows(one_hot, back_cols).astype(jnp.bfloat16)

    d_gate = contract_rows(rows_in, jnp.concatenate(grad_gate, axis=0))
    d_up = contract_rows(rows_in, jnp.concatenate(grad_up, axis=0))
    d_gate_up = jnp.stack([d_gate, d_up], axis=1)
    d_down = jnp.concatenate(
        [
            contract_rows(rows_cot, jnp.concatenate(scaled_left, axis=0)),
            contract_rows(rows_cot, jnp.concatenate(scaled_right, axis=0)),
        ],
        axis=1,
    )
    token_score = jnp.sum(jnp.where(placed, scores[:, None], 0.0), axis=0)
    d_combine = jnp.stack(
        [jnp.where(in_first, token_score, 0.0), jnp.where(in_second, token_score, 0.0)], axis=1
    )
    return (grad_tokens, d_combine, d_gate_up, d_down)


def solution(mesh):
    in_specs = (
        P("tok", "hid"),
        P("tok", "hid"),
        P("tok", None),
        P(),
        P("tok", None, "hid"),
        P("tok", "hid"),
    )
    out_specs = (P("tok", "hid"), P("tok", None), P("tok", None, "hid"), P("tok", "hid"))
    return jax.shard_map(local, mesh=mesh, in_specs=in_specs, out_specs=out_specs, check_vma=False)
```

```python
import jax
import jax.numpy as jnp
from jax import lax
from jax.sharding import PartitionSpec as P

CAP = 432


def silu_pair(pre):
    sigma = jax.nn.sigmoid(pre)
    return (pre * sigma, sigma * (1.0 + pre * (1.0 - sigma)))


def contract_rows(left, right):
    return lax.dot_general(
        left, right, (((0,), (0,)), ((), ())), preferred_element_type=jnp.float32
    )


def contract_cols(left, right):
    return lax.dot_general(
        left, right, (((1,), (1,)), ((), ())), preferred_element_type=jnp.float32
    )


def swap(value, bit):
    count = lax.axis_size("tok")
    return lax.ppermute(value, "tok", [(k, k ^ bit) for k in range(count)])


def after(value, *others):
    return lax.optimization_barrier((value, *others))[0]


def tok_sum(parts, bits, wire, late=None):
    held = dict(parts)
    for step, bit in enumerate(bits):
        sent = {j: held[j].astype(wire) for j in held if j & bit}
        if step == 1 and late is not None:
            late.extend(sent.values())
        arrived = {j ^ bit: swap(sent[j], bit) for j in sent}
        held = {j: held[j] + arrived[j].astype(jnp.float32) for j in held if not j & bit}
    return held[0]


def tok_gather(own, bits):
    held = {0: own}
    for bit in bits:
        held.update({j | bit: swap(held[j], bit) for j in list(held)})
    return [held[j] for j in range(lax.axis_size("tok"))]


def local(tokens, cotangent, expert_choice, router, gate_up, w_down):
    n_tok = lax.axis_size("tok")
    n_hid = lax.axis_size("hid")
    share = n_hid // n_tok
    local_cols = tokens.shape[1]
    weight_rows, hidden_local = w_down.shape
    half = hidden_local // 2
    ups = [1 << b for b in range((n_tok - 1).bit_length())]
    downs = ups[::-1]
    first = expert_choice[:, 0]
    second = expert_choice[:, 1]
    in_first = first == 0
    in_second = second == 0
    routed = jnp.logical_or(in_first, in_second)
    flags = routed.astype(jnp.int32)
    slot_rank = jnp.cumsum(flags) - flags
    slot_ids = jnp.arange(CAP, dtype=jnp.int32)
    placed = jnp.logical_and(routed[None, :], slot_rank[None, :] == slot_ids[:, None])
    one_hot = placed.astype(jnp.bfloat16)
    forth = [
        (k * n_hid + t * share + c, t * n_hid + c * n_tok + (k ^ t))
        for k in range(n_tok)
        for t in range(n_tok)
        for c in range(share)
    ]
    back_pairs = [(b, a) for a, b in forth]

    def pick(values):
        return jnp.dot(one_hot, values, preferred_element_type=jnp.float32).astype(jnp.bfloat16)

    def spread(moved):
        return lax.all_gather(moved, "hid", axis=0).reshape(share, n_tok, CAP, local_cols)

    def joined(pieces):
        flat = pieces.reshape(share, n_tok * CAP, local_cols)
        return jnp.concatenate([flat[c] for c in range(share)], axis=1)

    picked_in = pick(tokens)
    moved_in = lax.ppermute(picked_in, ("tok", "hid"), forth)
    picked_in, picked_cot, _ = lax.optimization_barrier((picked_in, pick(cotangent), moved_in))
    moved_cot = lax.ppermute(picked_cot, ("tok", "hid"), forth)
    pieces_in = spread(moved_in)
    router_cols = lax.dynamic_slice_in_dim(
        router, lax.axis_index("hid") * local_cols, local_cols, 1
    )
    logits = lax.psum(contract_cols(router_cols, picked_in), "hid")
    pieces_cot = spread(moved_cot)
    w_gate = gate_up[:, 0, :]
    w_up = gate_up[:, 1, :]

    def products(pieces, weights, order):
        def one(j):
            total = None
            for c in range(share):
                rows = weights[c * local_cols : (c + 1) * local_cols]
                term = jnp.dot(pieces[c, j], rows, preferred_element_type=jnp.float32)
                total = term if total is None else total + term
            return total

        return {j: one(j) for j in order}

    order = list(range(n_tok))
    late = []
    gate_pre = tok_sum(products(pieces_in, w_gate, order), ups, jnp.bfloat16, late)
    up_pre = tok_sum(products(pieces_in, w_up, order), downs, jnp.bfloat16, late)
    pieces_cot = after(pieces_cot, *late)
    raw = jnp.concatenate(
        [
            tok_sum(products(pieces_cot, w_down[:, :half], order), ups, jnp.bfloat16),
            tok_sum(products(pieces_cot, w_down[:, half:], order), downs, jnp.bfloat16),
        ],
        axis=1,
    )
    slot_other = jnp.sum(jnp.where(placed, (first + second)[None, :], 0), axis=1)
    filled = jnp.any(placed, axis=1)
    labels = jnp.arange(logits.shape[0], dtype=jnp.int32)
    other_logit = jnp.sum(jnp.where(slot_other[None, :] == labels[:, None], logits, 0.0), axis=0)
    slot_gate = jnp.where(filled, jax.nn.sigmoid(logits[0] - other_logit), 0.0)

    active, slope = silu_pair(gate_pre)
    product = active * up_pre
    scale = slot_gate[:, None]
    scaled = (scale * product).astype(jnp.bfloat16)
    score_part = jnp.sum(product * raw, axis=1)
    upstream = scale * raw
    own_gate = (upstream * up_pre * slope).astype(jnp.bfloat16)
    grad_gate = tok_gather(own_gate, ups)
    grad_up = tok_gather((upstream * active).astype(jnp.bfloat16), downs)
    scores = lax.psum(after(score_part, own_gate), "hid")
    scaled_left = tok_gather(scaled[:, :half], ups)
    scaled_right = tok_gather(scaled[:, half:], downs)

    rows_in, rows_cot = joined(pieces_in), joined(pieces_cot)
    held_gate = [grad_gate[0]] + [after(g, scores, rows_in, rows_cot) for g in grad_gate[1:]]
    backs = [
        (contract_cols(held_gate[j], w_gate) + contract_cols(grad_up[j], w_up)).astype(jnp.bfloat16)
        for j in range(n_tok)
    ]
    shares = jnp.stack(
        [
            backs[j][:, c * local_cols : (c + 1) * local_cols]
            for c in range(share)
            for j in range(n_tok)
        ]
    )
    reduced = lax.psum_scatter(shares, "hid", scatter_dimension=0, tiled=False)

    def stacked(left, right):
        parts = [jnp.concatenate([left[j], right[j]], axis=1) for j in range(n_tok)]
        return lax.optimization_barrier(jnp.concatenate(parts, axis=0))

    d_gate_up = contract_rows(rows_in, stacked(grad_gate, grad_up))
    d_gate_up = d_gate_up.reshape(weight_rows, 2, hidden_local)
    d_down = contract_rows(rows_cot, stacked(scaled_left, scaled_right))
    back_cols = lax.ppermute(after(reduced, d_gate_up), ("tok", "hid"), back_pairs)
    grad_tokens = contract_rows(one_hot, back_cols).astype(jnp.bfloat16)
    token_score = jnp.sum(jnp.where(placed, scores[:, None], 0.0), axis=0)
    d_combine = jnp.stack(
        [jnp.where(in_first, token_score, 0.0), jnp.where(in_second, token_score, 0.0)], axis=1
    )
    return (grad_tokens, d_combine, d_gate_up, d_down)


def solution(mesh):
    in_specs = (
        P("tok", "hid"),
        P("tok", "hid"),
        P("tok", None),
        P(),
        P("tok", None, "hid"),
        P("tok", "hid"),
    )
    out_specs = (P("tok", "hid"), P("tok", None), P("tok", None, "hid"), P("tok", "hid"))
    return jax.shard_map(local, mesh=mesh, in_specs=in_specs, out_specs=out_specs, check_vma=False)
```
